512 devices in a mesh: seq: 64 (over x, y, core), head: 8 (over z).
Axes of the slice: x: 4, y: 8, z: 8, core: 2. Of those that a mesh axis runs over, the one named last changes fastest.
Arguments:
- tokens: float32 [8192, 2048], P('seq'), may hold values from -45 to 45
- cluster: int32 [8192, 1], P('seq'), may hold values from 0 to 255; in each aligned block of 128 rows (0 to 127, 128 to 255, ...) at most 4 rows name the same one
- w_query: float32 [2048, 1024], P('seq', 'head'), may hold values from -0.125 to 0.125
- w_key: float32 [2048, 1024], P('seq', 'head'), may hold values from -0.125 to 0.125
- w_value: float32 [2048, 1024], P('seq', 'head'), may hold values from -0.125 to 0.125
- grad_out: float32 [8192, 1024], P('seq', 'head'), may hold values from -6 to 6
Outputs:
- attended: float32 [8192, 1024], P('seq', 'head')
- grad_query: float32 [2048, 1024], P('seq', 'head')
- grad_key: float32 [2048, 1024], P('seq', 'head')
- grad_value: float32 [2048, 1024], P('seq', 'head')
The draws below stay inside these ranges and needn't reach their ends.
Inputs may be any that keep to these rules, and one draw needn't show every extreme that they name: In the rows of one device (each aligned block of 128 rows), no cluster is named more than 4 times, a bound that some block reaches.
All inputs are finite; a program needn't handle non-finite values.
Results may differ from the reference program's by a relative error of at most 0.0003.
Values sent between devices are 32-bit elements; how exact they have to be, the bound alone decides.
A program may use at most 64 MiB of HBM per device.

```python
import math
import jax
import jax.numpy as jnp
import numpy as np
from jax import lax

D = 2048
HEADS = 8
HS = 128
CLUST_DEV = 4
CAP = 4
TOK_DEV = 128
TOKENS = 8192
CLUSTERS = 256
N_SEQ = 64


def draw_tokens(key, part):
    base_key = jax.random.fold_in(key, 11)
    scale_key = jax.random.fold_in(key, 12)
    base = jnp.clip(jax.random.normal(base_key, (TOKENS, D), jnp.float32), -4.5, 4.5)
    row_scale = jax.random.uniform(scale_key, (TOKENS, 1), jnp.float32, 0.7, 1.3)
    return base * row_scale


def levels(key, dims, pieces, smallest, top_value):
    level = 1.0
    for dim, blocks in pieces:
        heights = jax.random.uniform(jax.random.fold_in(jax.random.fold_in(key, 6), dim), (blocks,), jnp.float32, smallest / len(pieces), top_value / len(pieces))
        level = level * jnp.repeat(jnp.exp(heights), dims[dim] // blocks).reshape((-1,) + (1,) * (len(dims) - 1 - dim))
    return level


def assign_block(rng, own, number, rows, number_of, top, limit, lean):
    ranking = jax.random.permutation(rng, number_of)
    crowded, ordinary = load_shares(number_of, rows * top, limit, lean, True), load_shares(number_of, rows * top, limit, lean, False)
    places = jnp.arange(number_of)

    def named(tallies, rotation):
        used = int((tallies > 0).sum())
        fixed = max(1, used // 4)
        passed = fixed + (places - fixed + rotation * (used - fixed)) % max(1, number_of - fixed)
        return jnp.zeros((number_of,), jnp.int32).at[ranking[jnp.where(places < fixed, places, passed)]].set(jnp.asarray(tallies, jnp.int32))

    tallies = jnp.where(number % 4 == 0, named(crowded, number // 4), named(ordinary, number - number // 4 - 1))
    mixed = jax.random.permutation(jax.random.fold_in(own, 3), number_of)
    giver, sink = mixed[0:number_of // 2 * 2:2], mixed[1:number_of // 2 * 2:2]
    slack = jnp.minimum(tallies[giver] - 1, limit - tallies[sink]) // 2
    slack = jnp.where((giver == ranking[0]) | (sink == ranking[0]) | (tallies[sink] == 0), 0, jnp.maximum(slack, 0))
    passed = jax.random.randint(jax.random.fold_in(own, 4), (number_of // 2,), 0, 1 << 20) % (slack + 1)
    tallies = tallies.at[giver].add(-passed).at[sink].add(passed)
    labels = jnp.searchsorted(jnp.cumsum(tallies), jnp.arange(rows * top), side="right").astype(jnp.int32)
    grid = labels.reshape(top, rows).T
    grid = grid[jax.random.permutation(jax.random.fold_in(own, 1), rows)]
    rotation = jax.random.randint(jax.random.fold_in(own, 2), (rows, 1), 0, top)
    return jnp.take_along_axis(grid, (jnp.arange(top)[None, :] + rotation) % top, axis=1)


def load_shares(amount, total, bound, skew, full):
    portions = [(1 << 20) // math.isqrt(rank ** skew) + 1 for rank in range(1, amount + 1)]
    largest = bound if full else min(bound, max(-(-total // amount), total * portions[0] // sum(portions)))
    least = 1 if total - largest >= amount - 1 else 0
    counts, spare = [largest] + [least] * (amount - 1), total - largest - least * (amount - 1)
    while spare > 0:
        candidates = [i for i in range(1, amount) if counts[i] < largest] or [i for i in range(1, amount) if counts[i] < bound]
        whole, left = sum([portions[i] for i in candidates]), spare
        for i in candidates:
            addition = min(bound - counts[i], max(1, left * portions[i] // whole), spare)
            counts[i] = counts[i] + addition
            spare = spare - addition
    return np.array(counts)


def normal_values(stream_key, shape, deviation, reach, pieces=(), kind=jnp.bfloat16):
    level = levels(stream_key, shape, pieces, -0.22, 0.18) if pieces else 1.0
    values = jax.random.normal(stream_key, shape, jnp.float32) * deviation * level
    return jnp.minimum(jnp.maximum(values, -reach), reach).astype(kind)


def setup_inputs(seed: int = 0) -> dict:
    arg_keys = jax.random.split(jax.random.key(seed), 7)
    tokens = draw_tokens(jax.random.fold_in(arg_keys[6], 71), 0)
    cluster_keys = jax.random.split(jax.random.fold_in(arg_keys[1], 1), TOKENS // TOK_DEV)
    cluster_turns = jax.random.permutation(jax.random.fold_in(arg_keys[1], 3), TOKENS // TOK_DEV)
    cluster = jax.vmap(lambda own, number: assign_block(jax.random.fold_in(arg_keys[1], 2), own, number, TOK_DEV, CLUSTERS, 1, CAP, 2))(cluster_keys, cluster_turns).reshape((TOKENS, 1))
    w_query = normal_values(arg_keys[2], (D, HEADS * HS), D ** -0.5, 0.125, ((0, 64), (1, 8)), jnp.float32)
    w_key = normal_values(arg_keys[3], (D, HEADS * HS), D ** -0.5, 0.125, ((0, 64), (1, 8)), jnp.float32)
    w_value = normal_values(arg_keys[4], (D, HEADS * HS), D ** -0.5, 0.125, ((0, 64), (1, 8)), jnp.float32)
    grad_out = normal_values(arg_keys[5], (TOKENS, HEADS * HS), 1.0, 6.0, ((0, 64), (1, 8)), jnp.float32)
    return dict(tokens=tokens, cluster=cluster, w_query=w_query, w_key=w_key, w_value=w_value, grad_out=grad_out)


highest = lax.Precision.HIGHEST

def probabilities(query, key_rows, occupied, head_count):
    groups, length, width = query.shape
    query_h = query.reshape(groups, length, head_count, width // head_count)
    key_h = key_rows.reshape(groups, length, head_count, width // head_count)
    score_scale = 1.0 / math.sqrt(width // head_count)
    scores = jnp.einsum('cihd,cjhd->chij', query_h, key_h, precision=highest) * score_scale
    positions = jnp.arange(length)
    causal = positions[None, :] <= positions[:, None]
    allowed = causal[None] & (occupied[:, None, :] > 0.5) | jnp.eye(length, dtype=bool)[None]
    allowed = allowed[:, None]
    row_max = lax.optimization_barrier(jnp.max(jnp.where(allowed, scores, -1e+30), axis=-1, keepdims=True))
    shifted = jnp.where(allowed, scores - row_max, -1e+30)
    expos = jnp.exp(shifted)
    return expos / lax.optimization_barrier(jnp.sum(expos, axis=-1, keepdims=True))

def attend(query, key_rows, value_rows, occupied, head_count):
    groups, length, width = query.shape
    weights = probabilities(query, key_rows, occupied, head_count)
    value_h = value_rows.reshape(groups, length, head_count, width // head_count)
    result = jnp.einsum('chij,cjhd->cihd', weights, value_h, precision=highest)
    return result.reshape(groups, length, width)

def slot_numbers(cluster):
    cluster_ids = cluster[:, 0].reshape(N_SEQ, TOK_DEV).astype(jnp.int32)
    onehot = (cluster_ids[:, :, None] == jnp.arange(CLUSTERS, dtype=jnp.int32)[None, None, :]).astype(jnp.int32)
    before = jnp.cumsum(onehot, axis=1) - onehot
    rank_in = lax.optimization_barrier(jnp.sum(onehot * before, axis=-1)).astype(jnp.int32)
    return (cluster_ids * CAP + rank_in).astype(jnp.int32)

def reference(tokens, cluster, w_query, w_key, w_value, grad_out):
    slot_index = slot_numbers(cluster)
    sources = jnp.arange(N_SEQ, dtype=jnp.int32)[:, None]
    width = w_query.shape[1]
    length = N_SEQ * CAP

    def to_owner(rows):
        buffer = jnp.zeros((N_SEQ, CLUSTERS * CAP, width), rows.dtype)
        buffer = buffer.at[sources, slot_index].set(rows.reshape(N_SEQ, TOK_DEV, width))
        buffer = buffer.reshape(N_SEQ, CLUSTERS, CAP, width).transpose(1, 0, 2, 3)
        return buffer.reshape(N_SEQ, CLUST_DEV, length, width)
    occupied = jnp.zeros((N_SEQ, CLUSTERS * CAP), jnp.float32).at[sources, slot_index].set(1.0)
    occupied = occupied.reshape(N_SEQ, CLUSTERS, CAP).transpose(1, 0, 2).reshape(N_SEQ, CLUST_DEV, length)

    def from_owner(buffer):
        buffer = buffer.reshape(CLUSTERS, N_SEQ, CAP, width).transpose(1, 0, 2, 3)
        buffer = buffer.reshape(N_SEQ, CLUSTERS * CAP, width)
        return buffer[sources, slot_index].reshape(TOKENS, width)

    def forward(weight_q, weight_k, weight_v):
        query = to_owner(jnp.dot(tokens, weight_q, precision=highest, preferred_element_type=jnp.float32))
        key_rows = to_owner(jnp.dot(tokens, weight_k, precision=highest, preferred_element_type=jnp.float32))
        value_rows = to_owner(jnp.dot(tokens, weight_v, precision=highest, preferred_element_type=jnp.float32))

        def one_owner(group):
            return attend(group[0], group[1], group[2], group[3], HEADS)
        owner_out = lax.map(one_owner, (query, key_rows, value_rows, occupied))
        return from_owner(owner_out)
    attended, pullback = jax.vjp(forward, w_query, w_key, w_value)
    grads = pullback(grad_out)
    return (attended, grads[0], grads[1], grads[2])
```

```python
import functools
import math

import jax
import jax.numpy as jnp
from jax import lax
from jax.experimental import pallas as pl
from jax.experimental.pallas import tpu as pltpu
from jax.sharding import PartitionSpec as P

MESH = pl.DeviceIdType.MESH
F32 = jnp.float32
BF16 = jnp.bfloat16
X, Y, C = 4, 8, 2
T = 128
H = 128
D = 2048
SCALE = 1.0 / math.sqrt(H)
NEG = -1e30
COPIES = 256

NT = ((1,), (1,))
NN = ((1,), (0,))


def split(a):
    hi = a.astype(BF16)
    return hi, (a - hi.astype(F32)).astype(BF16)


def dot3(a, b, dims):
    def one(p, q):
        return lax.dot_general(p, q, (dims, ((), ())), preferred_element_type=F32)

    return one(a[0], b[0]) + (one(a[0], b[1]) + one(a[1], b[0]))


def kernel(
    tok_in, clu, wq, wk, wv, gout,
    att_o, grad_o,
    tok, wbuf, tokh, tokl, toth, totl, qb, gb, kv, cq, ck, ckb, pkb,
    kvh, kvl, kth, ktl, qgh, qgl, eb, gvb, ph, pl_, dh, dl, stb, al_s, rr_s,
    ob, obr, obl, gqb, gq_in, gq_half, gkv, gsib, gx, gw, gws, ga_r, ga_l, gbx, gb_r, gb_l, gax,
    send, recv, here,
):
    me = lax.axis_index("seq")
    c = lax.rem(me, C)
    y = lax.rem(me // C, Y)
    x = me // (C * Y)

    def yy(d):
        return lax.rem(y + (d + 2 * Y), Y)

    def xx(d):
        return lax.rem(x + (d + 2 * X), X)

    def dev(xd, yd, cd):
        return (xd * Y + yd) * C + cd

    right, left, sib = dev(x, yy(1), c), dev(x, yy(-1), c), dev(x, y, 1 - c)
    along = (1, right, 0), (-1, left, 1)
    copies = []

    def start(src, dst, device):
        i = len(copies)
        copy = pltpu.make_async_remote_copy(
            src_ref=src, dst_ref=dst, send_sem=send.at[i], recv_sem=recv.at[i],
            device_id={"seq": device}, device_id_type=MESH,
        )
        copy.start()
        copies.append(copy)
        return copy

    def share(ref, device):
        return start(ref, ref, device)

    near = [right, left, sib] + [dev(xx(d), y, c) for d in range(1, X)]
    barrier = pltpu.get_barrier_semaphore()
    for peer in near:
        pl.semaphore_signal(barrier, inc=1, device_id={"seq": peer}, device_id_type=MESH)

    local_copies = []

    def fetch(src, dst):
        copy = pltpu.make_async_copy(src, dst, here.at[len(local_copies)])
        copy.start()
        local_copies.append(copy)

    for half in range(2):
        for i, ref in enumerate((wq, wk, wv)):
            fetch(ref.at[pl.ds(half * 16, 16), :], wbuf.at[x, y, c, half, :, pl.ds(i * H, H)])
    fetch(gout, gb.at[y])
    fetch(tok_in, tok)
    ids = jnp.broadcast_to(clu[...].astype(F32), (8, T))
    cq[y] = ids
    ck[x, c] = ids
    for copy in local_copies[:6]:
        copy.wait()
    pl.semaphore_wait(barrier, len(near))

    class Gather:
        def __init__(self, slot, half):
            self.slot, self.half = slot, half
            self.sent = [[share(slot(y), to)] for _, to, _ in along]

        def step(self, k):
            for (sign, to, h), sent in zip(along, self.sent):
                sent[k - 1].wait_recv()
                if k < 4:
                    o = yy(-sign * k)
                    sent.append(share(self.slot(o) if k < 3 else self.half(o, h), to))

    class Scatter:
        def __init__(self, part, half, into, into_half):
            self.part, self.half, self.into, self.into_half = part, half, into, into_half
            self.sent = [[start(half(yy(4), h), into_half[h], to)] for _, to, h in along]

        def step(self, k):
            for (sign, to, h), sent in zip(along, self.sent):
                sent[k - 1].wait_recv()
                o = yy(sign * (4 - k))
                mine = self.part(o)
                if k == 1:
                    first = self.half(o, h)
                    first[...] += self.into_half[h][...]
                else:
                    mine[...] += self.into(h, k - 1)[...]
                if k < 4:
                    sent.append(start(mine, self.into(h, k), to))

    def arrived(k):
        return (yy(0),) if k == 0 else ((yy(4),) if k == 4 else (yy(-k), yy(k)))

    def ring_for(xo):
        return Gather(lambda o: wbuf.at[xo, o, c, 0], lambda o, h: wbuf.at[xo, o, c, 0, pl.ds(8 * h, 8)])

    a_x = {d: share(wbuf.at[x, y, c, 0], dev(xx(d), y, c)) for d in (1, 3, 2)}
    rings = [ring_for(x)]
    ring_b = Gather(lambda o: wbuf.at[x, o, c, 1], lambda o, h: wbuf.at[x, o, c, 1, pl.ds(8 * h, 8)])
    b_x = {}
    from_sib = []

    def spread(k):
        b_x[k] = [(o, [share(wbuf.at[x, o, c, 1], dev(xx(d), y, c)) for d in (1, 3, 2)]) for o in arrived(k)]

    def across(k):
        for o, landed in b_x[k]:
            for copy in landed:
                copy.wait_recv()
            from_sib.append(share(wbuf.at[:, o, c, 1], sib))

    spread(0)
    local_copies[7].wait()

    def halves(i, _):
        cols = pl.ds(pl.multiple_of(i * 128, 128), 128)
        block = tok[:, cols]
        hi, lo = split(block)
        tokh[:, cols] = hi
        tokl[:, cols] = lo
        hi, lo = split(jnp.transpose(block))
        toth[cols, :] = hi
        totl[cols, :] = lo
        return 0

    lax.fori_loop(0, 6, halves, 0)
    for d in (1, 3, 2):
        a_x[d].wait_recv()
        rings.append(ring_for(xx(-d)))
    from_sib.append(share(wbuf.at[:, y, c, 0], sib))
    local_copies[6].wait()
    for k in range(1, 5):
        rings[0].step(k)
        ring_b.step(k)
        spread(k)
        if k == 1:
            ring_g = Gather(lambda o: gb.at[o], lambda o, h: gb.at[o, pl.ds(64 * h, 64)])
        for ring in rings[1:]:
            ring.step(k)
        for o in arrived(k):
            from_sib.append(share(wbuf.at[:, o, c, 0], sib))
        if k > 1:
            ring_g.step(k - 1)
        across(k - 1)
        lax.fori_loop(3 + 3 * k, min(6 + 3 * k, D // 128), halves, 0)
    across(4)
    for copy in from_sib:
        copy.wait_recv()

    qkv = None
    for i in range(X):
        w = split(wbuf[i].reshape(D // X, 3 * H))
        cols = slice(i * (D // X), (i + 1) * (D // X))
        term = dot3((tokh[:, cols], tokl[:, cols]), w, NN)
        qkv = term if qkv is None else qkv + term
    qb[y] = qkv[:, 0:H]
    kv[0, x, c] = qkv[:, H:2 * H]
    kv[1, x, c] = qkv[:, 2 * H:]

    kv_x = {d: share(kv.at[:, x, c], dev(xx(d), y, c)) for d in (2, 1, 3)}
    kv_s = [share(kv.at[:, x, c], sib)]
    two = [share(qb.at[y], dev(x, yy(2 * sign), c)) for sign, _, _ in along]
    q_in = [share(qb.at[y], to) for _, to, _ in along]
    ids_in = [share(ck.at[x, c], dev(xx(d), y, c)) for d in range(1, X)]
    ids_in += [share(ck.at[x, c], dev(xx(d), y, 1 - c)) for d in range(X)]
    ids_in += [share(cq.at[y], dev(x, yy(d), c)) for d in range(1, Y)]

    def sides(xo, co):
        rows = pl.ds(pl.multiple_of((xo * C + co) * T, T), T)
        for n in range(2):
            block = kv[n, xo, co]
            hi, lo = split(block)
            kvh[n, rows, :] = hi
            kvl[n, rows, :] = lo
            hi, lo = split(jnp.transpose(block))
            kth[n, :, rows] = hi
            ktl[n, :, rows] = lo

    sides(x, c)
    kv_s[0].wait_recv()
    sides(x, 1 - c)
    for (sign, to, h), copy in zip(along, two):
        copy.wait_recv()
        o = yy(-2 * sign)
        q_in.append(share(qb.at[o, pl.ds(64 * h, 64)], dev(x, yy(2 * sign), c)))
        q_in.append(share(qb.at[o], to))
    ring_g.step(4)
    for copy in ids_in:
        copy.wait_recv()

    def keys(i, _):
        xo, co = i // C, lax.rem(i, C)
        ckb[i] = jnp.transpose(jnp.broadcast_to(ck[xo, co][0:1, :], (T, T)))
        pkb[i] = dev(xo, y, co) * T + lax.broadcasted_iota(jnp.int32, (T, T), 0)
        return 0

    lax.fori_loop(0, X * C, keys, 0)
    for d in (1, 3, 2):
        kv_x[d].wait_recv()
        kv_s.append(share(kv.at[:, xx(-d), c], sib))
        sides(xx(-d), c)
    for d, copy in zip((1, 3, 2), kv_s[1:]):
        copy.wait_recv()
        sides(xx(-d), 1 - c)
    for copy in q_in:
        copy.wait_recv()

    KEYS = X * C * T

    def forward(i, _):
        q = split(qb[pl.ds(2 * i, 2)].reshape(2 * T, H))
        g = split(gb[pl.ds(2 * i, 2)].reshape(2 * T, H))
        qgh[0, i], qgl[0, i] = q
        qgh[1, i], qgl[1, i] = g
        s = dot3((kvh[0], kvl[0]), q, NT) * SCALE
        gv = dot3((kvh[1], kvl[1]), g, NT)
        for n in range(2):
            o = 2 * i + n
            lanes = slice(n * T, (n + 1) * T)
            position = dev(x, o, c) * T + lax.broadcasted_iota(jnp.int32, (1, T), 1)
            same = ckb[...].reshape(KEYS, T) == cq[o][0:1, :]
            allowed = same & (pkb[...].reshape(KEYS, T) <= position)
            masked = jnp.where(allowed, s[:, lanes], NEG)
            top = jnp.max(masked, axis=0, keepdims=True)
            e = jnp.where(allowed, jnp.exp(masked - top), 0.0)
            gvn = gv[:, lanes]
            eb[o] = e
            gvb[o] = gvn
            stb[y, 0, pl.ds(o, 1), :] = top
            stb[y, 1, pl.ds(o, 1), :] = jnp.sum(e, axis=0, keepdims=True)
            stb[y, 2, pl.ds(o, 1), :] = jnp.sum(e * gvn, axis=0, keepdims=True)
        return 0

    lax.fori_loop(0, Y // 2, forward, 0)

    stats = [share(stb.at[y], dev(x, yy(d), c)) for d in (4, 3, 5, 2, 6, 1, 7)]
    for copy in stats:
        copy.wait_recv()
    top = stb[0, 0]
    for o in range(1, Y):
        top = jnp.maximum(top, stb[o, 0])
    total = jnp.zeros_like(top)
    row = jnp.zeros_like(top)
    for o in range(Y):
        factor = jnp.exp(stb[o, 0] - top)
        total = total + stb[o, 1] * factor
        row = row + stb[o, 2] * factor
    al_s[...] = jnp.exp(stb[y, 0] - top) / total
    rr_s[...] = row / total

    def softmax(i, _):
        for n in range(2):
            o = 2 * i + n
            lanes = slice(n * T, (n + 1) * T)
            p = eb[o] * al_s[pl.ds(o, 1), :]
            ph[i, :, lanes], pl_[i, :, lanes] = split(p)
            dh[i, :, lanes], dl[i, :, lanes] = split(p * ((gvb[o] - rr_s[pl.ds(o, 1), :]) * SCALE))
        return 0

    lax.fori_loop(0, Y // 2, softmax, 0)

    def key_side(xo):
        rows = pl.ds(pl.multiple_of(xo * (C * T), C * T), C * T)
        for n, (hi, lo) in enumerate(((dh, dl), (ph, pl_))):
            def add(i, acc):
                return acc + dot3((hi[i, rows, :], lo[i, rows, :]), (qgh[n, i], qgl[n, i]), NN)

            acc = lax.fori_loop(0, Y // 2, add, jnp.zeros((C * T, H), F32))
            gkv[n, xo] = acc.reshape(C, T, H)
        return start(gkv.at[:, xo, 1 - c], gsib.at[:, xo], sib)

    def query_side(n, hi, lo, into):
        def body(i, _):
            r = dot3((kth[n], ktl[n]), (hi[i], lo[i]), NN)
            into[2 * i] = r[:, 0:T]
            into[2 * i + 1] = r[:, T:]
            return 0

        lax.fori_loop(0, Y // 2, body, 0)

    sib_in = {2: key_side(xx(2))}
    query_side(0, dh, dl, gqb)
    gq_4 = [start(gqb.at[yy(4), pl.ds(64 * h, 64)], gq_half.at[h], dev(x, yy(2 * sign), c)) for sign, _, h in along]
    gq_3 = [start(gqb.at[yy(3 * sign)], gq_in.at[h, 0], to) for sign, to, h in along]
    gq_1 = [start(gqb.at[yy(sign)], gq_in.at[h, 1], to) for sign, to, h in along]
    x_in = []

    def key_send(d):
        sib_in[d].wait_recv()
        gkv[:, xx(d), c] += gsib[:, xx(d)]
        if d:
            x_in.append(start(gkv.at[:, xx(d), c], gx.at[d - 1], dev(xx(d), y, c)))

    for d, last in ((1, 2), (3, 1), (0, 3)):
        sib_in[d] = key_side(xx(d))
        key_send(last)
    gq_2 = []
    for (sign, to, h), far, near_ in zip(along, gq_4, gq_3):
        o = yy(2 * sign)
        far.wait_recv()
        gqb[o, 64 * h:64 * h + 64, :] += gq_half[h]
        near_.wait_recv()
        gqb[o] += gq_in[h, 0]
        gq_2.append(start(gqb.at[o], gq_in.at[h, 2], dev(x, yy(2 * sign), c)))
    query_side(1, ph, pl_, ob)
    ring_o = Scatter(
        lambda o: ob.at[o], lambda o, h: ob.at[o, pl.ds(64 * h, 64)],
        lambda h, k: (obr, obl)[h].at[k], (obr.at[0, pl.ds(0, 64)], obl.at[0, pl.ds(64, 64)]),
    )
    key_send(0)
    for copy in gq_1 + gq_2 + x_in:
        copy.wait_recv()
    gq = (gqb[y] + (gq_in[0, 1] + gq_in[1, 1])) + (gq_in[0, 2] + gq_in[1, 2])
    parts = [jnp.transpose(gq)]
    for n in range(2):
        parts.append((gkv[n, x, c] + gx[0, n]) + (gx[1, n] + gx[2, n]))
    grads = split(jnp.concatenate(parts, axis=1))

    far_first = (2, 1, 3, 0)
    y_order = (4, 3, -3, 2, -2, 1, -1, 0)

    def project(d):
        xo = xx(d)
        rows = pl.ds(pl.multiple_of(xo * (D // X), D // X), D // X)
        gw[xo] = dot3((toth[rows, :], totl[rows, :]), grads, NN).reshape(Y, C, 2, 16, 3 * H)
        return start(gw.at[xo, :, 1 - c], gws.at[xo], sib)

    def sum_ring(d):
        xo = xx(d)
        return Scatter(
            lambda o: gw.at[xo, o, c, 0], lambda o, h: gw.at[xo, o, c, 0, pl.ds(8 * h, 8)],
            lambda h, k: (ga_r, ga_l)[h].at[d, k], (ga_r.at[d, 0, pl.ds(0, 8)], ga_l.at[d, 0, pl.ds(8, 8)]),
        )

    sums = {}
    bx_in = {}

    def launch(d, copy):
        copy.wait_recv()
        xo = xx(d)
        gw[xo, :, c] += gws[xo]
        sums[d] = sum_ring(d)
        if d:
            for n in y_order:
                o = yy(n)
                bx_in[d, n] = start(gw.at[xo, o, c, 1], gbx.at[d - 1, o], dev(xo, y, c))

    last = None
    for d in far_first:
        copy = project(d)
        if last is not None:
            launch(*last)
        last = (d, copy)
    launch(*last)

    def gathered(*numbers):
        for n in numbers:
            o = yy(n)
            for d in range(1, X):
                bx_in[d, n].wait_recv()
            gw[x, o, c, 1] += (gbx[0, o] + gbx[1, o]) + gbx[2, o]

    sums[2].step(1)
    gathered(4)
    ring_b = Scatter(
        lambda o: gw.at[x, o, c, 1], lambda o, h: gw.at[x, o, c, 1, pl.ds(8 * h, 8)],
        lambda h, k: (gb_r, gb_l)[h].at[k], (gb_r.at[0, pl.ds(0, 8)], gb_l.at[0, pl.ds(8, 8)]),
    )
    a_in = []
    for k in range(1, 5):
        for d in far_first:
            if (d, k) != (2, 1):
                sums[d].step(k)
            if k == 4 and d:
                a_in.append(start(gw.at[xx(d), y, c, 0], gax.at[d - 1], dev(xx(d), y, c)))
        gathered(*((4 - k, k - 4) if k < 4 else (0,)))
        ring_b.step(k)
        ring_o.step(k)
    att_o[...] = jnp.transpose(ob[y])
    grad_o[16:32, :] = gw[x, y, c, 1]
    for copy in a_in:
        copy.wait_recv()
    grad_o[0:16, :] = (gw[x, y, c, 0] + gax[0]) + (gax[1] + gax[2])
    for copy in copies:
        copy.wait_send()


def results(att, grad, att_o, gq_o, gk_o, gv_o):
    att_o[...] = att[...]
    for i, ref in enumerate((gq_o, gk_o, gv_o)):
        ref[...] = grad[:, i * H:(i + 1) * H]


def local(tokens, cluster, w_query, w_key, w_value, grad_out):
    vmem = pl.BlockSpec(memory_space=pltpu.VMEM)
    hbm = pl.BlockSpec(memory_space=pl.ANY)
    W3 = 3 * H
    keys = X * C * T
    pairs = Y // 2
    scratch = [
        pltpu.VMEM((T, D), F32),
        pltpu.VMEM((X, Y, C, 2, 16, W3), F32),
        pltpu.VMEM((T, D), BF16), pltpu.VMEM((T, D), BF16),
        pltpu.VMEM((D, T), BF16), pltpu.VMEM((D, T), BF16),
        pltpu.VMEM((Y, T, H), F32), pltpu.VMEM((Y, T, H), F32),
        pltpu.VMEM((2, X, C, T, H), F32),
        pltpu.VMEM((Y, 8, T), F32), pltpu.VMEM((X, C, 8, T), F32),
        pltpu.VMEM((X * C, T, T), F32), pltpu.VMEM((X * C, T, T), jnp.int32),
        pltpu.VMEM((2, keys, H), BF16), pltpu.VMEM((2, keys, H), BF16),
        pltpu.VMEM((2, H, keys), BF16), pltpu.VMEM((2, H, keys), BF16),
        pltpu.VMEM((2, pairs, 2 * T, H), BF16), pltpu.VMEM((2, pairs, 2 * T, H), BF16),
        pltpu.VMEM((Y, keys, T), F32), pltpu.VMEM((Y, keys, T), F32),
        pltpu.VMEM((pairs, keys, 2 * T), BF16), pltpu.VMEM((pairs, keys, 2 * T), BF16),
        pltpu.VMEM((pairs, keys, 2 * T), BF16), pltpu.VMEM((pairs, keys, 2 * T), BF16),
        pltpu.VMEM((Y, 3, Y, T), F32),
        pltpu.VMEM((Y, T), F32), pltpu.VMEM((Y, T), F32),
        pltpu.VMEM((Y, H, T), F32),
        pltpu.VMEM((4, H, T), F32), pltpu.VMEM((4, H, T), F32),
        pltpu.VMEM((Y, H, T), F32),
        pltpu.VMEM((2, 3, H, T), F32), pltpu.VMEM((2, H // 2, T), F32),
        pltpu.VMEM((2, X, C, T, H), F32),
        pltpu.VMEM((2, X, T, H), F32),
        pltpu.VMEM((X - 1, 2, T, H), F32),
        pltpu.VMEM((X, Y, C, 2, 16, W3), F32),
        pltpu.VMEM((X, Y, 2, 16, W3), F32),
        pltpu.VMEM((X, 4, 16, W3), F32), pltpu.VMEM((X, 4, 16, W3), F32),
        pltpu.VMEM((X - 1, Y, 16, W3), F32),
        pltpu.VMEM((4, 16, W3), F32), pltpu.VMEM((4, 16, W3), F32),
        pltpu.VMEM((X - 1, 16, W3), F32),
        pltpu.SemaphoreType.DMA((COPIES,)),
        pltpu.SemaphoreType.DMA((COPIES,)),
        pltpu.SemaphoreType.DMA((8,)),
    ]
    att, grad = pl.pallas_call(
        kernel,
        out_shape=(
            jax.ShapeDtypeStruct((T, H), F32),
            jax.ShapeDtypeStruct((D // 64, W3), F32),
        ),
        in_specs=[hbm, vmem, hbm, hbm, hbm, hbm],
        out_specs=(vmem,) * 2,
        scratch_shapes=scratch,
        compiler_params=pltpu.CompilerParams(
            collective_id=0, has_side_effects=True, vmem_limit_bytes=58 * 1024 * 1024
        ),
        name="routing",
    )(tokens, cluster.reshape(1, T), w_query, w_key, w_value, grad_out)
    part = jax.ShapeDtypeStruct((D // 64, H), F32)
    return pl.pallas_call(
        results,
        out_shape=(jax.ShapeDtypeStruct((T, H), F32), part, part, part),
        in_specs=[vmem] * 2,
        out_specs=(vmem,) * 4,
        name="results",
    )(att, grad)


def solution(mesh):
    in_specs = (P("seq", None), P("seq", None)) + (P("seq", "head"),) * 4
    out_specs = (P("seq", "head"),) * 4
    return jax.shard_map(local, mesh=mesh, in_specs=in_specs, out_specs=out_specs, check_vma=False)
```

```python
import functools
import math

import jax
import jax.numpy as jnp
from jax import lax
from jax.experimental import pallas as pl
from jax.experimental.pallas import tpu as pltpu
from jax.sharding import PartitionSpec as P

MESH = pl.DeviceIdType.MESH
F32 = jnp.float32
BF16 = jnp.bfloat16
X, Y, C = 4, 8, 2
T = 128
H = 128
D = 2048
SCALE = 1.0 / math.sqrt(H)
NEG = -1e30
COPIES = 136
ROWS = 8192

NT = ((1,), (1,))
NN = ((1,), (0,))


def split(a):
    hi = a.astype(BF16)
    return hi, (a - hi.astype(F32)).astype(BF16)


def dot3(a, b, dims):
    def one(p, q):
        return lax.dot_general(p, q, (dims, ((), ())), preferred_element_type=F32)

    return one(a[0], b[0]) + (one(a[0], b[1]) + one(a[1], b[0]))


def kernel(
    tok_in, clu, wq, wk, wv, gout,
    att_o, grad_o,
    tok, wbuf, tokh, tokl, toth, totl, qb, gb, kv, cq, ck, ckb, pkb,
    kvc, kvt, qsc, gsc, eb, gvb, eh, el, dh, dl, mlb, rb, al_s, rr_s,
    ob, obr, obl, gqb, gq_in, gq_half, gkv, gsib, gx, gw, gws, ga_r, ga_l, gbx, gb_r, gb_l, gax,
    sizer, send, recv, here,
):
    me = lax.axis_index("seq")
    c = lax.rem(me, C)
    y = lax.rem(me // C, Y)
    x = me // (C * Y)

    def yy(d):
        return lax.rem(y + (d + 2 * Y), Y)

    def xx(d):
        return lax.rem(x + (d + 2 * X), X)

    def dev(xd, yd, cd):
        return (xd * Y + yd) * C + cd

    right, left, sib = dev(x, yy(1), c), dev(x, yy(-1), c), dev(x, y, 1 - c)
    along = (1, right, 0), (-1, left, 1)
    groups = []
    sends = [0]

    class Batch:
        def __init__(self):
            self.rows, self.i = 0, len(groups)
            groups.append(self)

        def start(self, src, dst, device):
            rows = math.prod(src.shape) // 128
            if sends[-1] + rows > ROWS:
                sends.append(0)
            pltpu.make_async_remote_copy(
                src_ref=src, dst_ref=dst, send_sem=send.at[len(sends) - 1], recv_sem=recv.at[self.i],
                device_id={"seq": device}, device_id_type=MESH,
            ).start()
            sends[-1] += rows
            self.rows += rows
            return self

        def share(self, ref, device):
            return self.start(ref, ref, device)

        def wait_recv(self):
            some = sizer.at[pl.ds(0, self.rows)]
            pltpu.make_async_copy(some, some, recv.at[self.i]).wait()

    def start(src, dst, device):
        return Batch().start(src, dst, device)

    def share(ref, device):
        return Batch().share(ref, device)

    near = [dev(x, yy(d), c) for d in (1, -1, 2, -2)] + [dev(xx(d), y, c) for d in range(1, X)] + [sib]
    barrier = pltpu.get_barrier_semaphore()
    for peer in near:
        pl.semaphore_signal(barrier, inc=1, device_id={"seq": peer}, device_id_type=MESH)

    local_copies = []

    def fetch(src, dst):
        copy = pltpu.make_async_copy(src, dst, here.at[len(local_copies)])
        copy.start()
        local_copies.append(copy)

    for half in range(2):
        for i, ref in enumerate((wq, wk, wv)):
            fetch(ref.at[pl.ds(half * 16, 16), :], wbuf.at[x, y, c, half, :, pl.ds(i * H, H)])
    fetch(gout, gb.at[y])
    fetch(tok_in, tok)
    ids = jnp.broadcast_to(clu[...].astype(F32), (8, T))
    cq[y] = ids
    ck[x, c] = ids
    for copy in local_copies[:6]:
        copy.wait()
    pl.semaphore_wait(barrier, len(near))

    class Gather:
        def __init__(self, slots, halves):
            self.slots, self.halves = slots, halves
            self.two = [self.share(slots(y), dev(x, yy(2 * sign), c)) for sign, _, _ in along]
            self.one = [self.share(slots(y), to) for _, to, _ in along]

        def share(self, refs, device):
            batch = Batch()
            for ref in refs:
                batch.share(ref, device)
            return batch

        def step(self):
            self.far = []
            for (sign, to, h), copy in zip(along, self.two):
                copy.wait_recv()
                o = yy(-2 * sign)
                self.far.append(self.share(self.halves(o, h), dev(x, yy(2 * sign), c)))
                self.far.append(self.share(self.slots(o), to))
            for copy in self.one:
                copy.wait_recv()

        def finish(self):
            for copy in self.far:
                copy.wait_recv()

    class Sum:
        def __init__(self, parts, halves, into, into_half):
            self.parts, self.halves, self.into, self.into_half = parts, halves, into, into_half
            self.four = [
                self.start(halves(yy(4), h), into_half(h), dev(x, yy(2 * sign), c)) for sign, _, h in along
            ]
            self.three = [self.start(parts(yy(3 * sign)), into(h, 0), to) for sign, to, h in along]

        def start(self, src, dst, device):
            batch = Batch()
            for a, b in zip(src, dst):
                batch.start(a, b, device)
            return batch

        def step(self):
            self.two = []
            for (sign, _, h), four, three in zip(along, self.four, self.three):
                o = yy(2 * sign)
                four.wait_recv()
                for a, b in zip(self.halves(o, h), self.into_half(h)):
                    a[...] += b[...]
                three.wait_recv()
                for a, b in zip(self.parts(o), self.into(h, 0)):
                    a[...] += b[...]
                self.two.append(self.start(self.parts(o), self.into(h, 2), dev(x, yy(2 * sign), c)))

        def near(self):
            self.one = [self.start(self.parts(yy(sign)), self.into(h, 1), to) for sign, to, h in along]

        def finish(self):
            for copy in self.one + self.two:
                copy.wait_recv()
            for k in (1, 2):
                for h in (0, 1):
                    for a, b in zip(self.parts(y), self.into(h, k)):
                        a[...] += b[...]

    class Scatter:
        def __init__(self, part, half, into, into_half):
            self.part, self.half, self.into, self.into_half = part, half, into, into_half
            self.sent = [[start(half(yy(4), h), into_half[h], to)] for _, to, h in along]

        def step(self, k):
            for (sign, to, h), sent in zip(along, self.sent):
                sent[k - 1].wait_recv()
                o = yy(sign * (4 - k))
                mine = self.part(o)
                if k == 1:
                    first = self.half(o, h)
                    first[...] += self.into_half[h][...]
                else:
                    mine[...] += self.into(h, k - 1)[...]
                if k < 4:
                    sent.append(start(mine, self.into(h, k), to))

    def tree_for(*xs):
        return Gather(
            lambda o: [wbuf.at[i, o, c, 0] for i in xs],
            lambda o, h: [wbuf.at[i, o, c, 0, pl.ds(8 * h, 8)] for i in xs],
        )

    a_x = Batch()
    for d in (1, 3, 2):
        a_x.share(wbuf.at[x, y, c, 0], dev(xx(d), y, c))
    tree_own = tree_for(x)
    tree_b = Gather(lambda o: [wbuf.at[x, o, c, 1]], lambda o, h: [wbuf.at[x, o, c, 1, pl.ds(8 * h, 8)]])
    b_x = []
    sib_a, sib_b = Batch(), Batch()

    def spread(*numbers):
        for n in numbers:
            o, batch = yy(n), Batch()
            for d in (1, 3, 2):
                batch.share(wbuf.at[x, o, c, 1], dev(xx(d), y, c))
            b_x.append((o, batch))

    def across(count):
        for o, batch in b_x[:count]:
            batch.wait_recv()
            sib_b.share(wbuf.at[:, o, c, 1], sib)
        del b_x[:count]

    def over(*numbers):
        for n in numbers:
            sib_a.share(wbuf.at[:, yy(n), c, 0], sib)

    spread(0)
    local_copies[7].wait()

    def halves(i, _):
        cols = pl.ds(pl.multiple_of(i * 128, 128), 128)
        block = tok[:, cols]
        hi, lo = split(block)
        tokh[:, cols] = hi
        tokl[:, cols] = lo
        hi, lo = split(jnp.transpose(block))
        toth[cols, :] = hi
        totl[cols, :] = lo
        return 0

    lax.fori_loop(0, 8, halves, 0)
    local_copies[6].wait()
    a_x.wait_recv()
    tree_rest = tree_for(*[xx(d) for d in range(1, X)])
    over(0)
    tree_own.step()
    tree_b.step()
    spread(2, -2, 1, -1)
    lax.fori_loop(8, 12, halves, 0)
    across(1)
    tree_own.finish()
    tree_b.finish()
    spread(3, -3, 4)
    tree_rest.step()
    tree_g = Gather(lambda o: [gb.at[o]], lambda o, h: [gb.at[o, pl.ds(64 * h, 64)]])
    over(1, -1, 2, -2)
    across(4)
    lax.fori_loop(12, D // 128, halves, 0)
    tree_rest.finish()
    over(3, -3, 4)
    across(3)
    sib_a.wait_recv()
    sib_b.wait_recv()

    qkv = None
    for i in range(X):
        w = split(wbuf[i].reshape(D // X, 3 * H))
        cols = slice(i * (D // X), (i + 1) * (D // X))
        term = dot3((tokh[:, cols], tokl[:, cols]), w, NN)
        qkv = term if qkv is None else qkv + term
    qb[y] = qkv[:, 0:H]
    kv[0, x, c] = qkv[:, H:2 * H]
    kv[1, x, c] = qkv[:, 2 * H:]

    def spread_keys(n):
        across_x = {d: share(kv.at[n, x, c], dev(xx(d), y, c)) for d in (2, 1, 3)}
        return across_x, share(kv.at[n, x, c], sib)

    k_x, k_own = spread_keys(0)
    tree_q = Gather(lambda o: [qb.at[o]], lambda o, h: [qb.at[o, pl.ds(64 * h, 64)]])
    ids_in = Batch()
    for d in range(X):
        if d:
            ids_in.share(ck.at[x, c], dev(xx(d), y, c))
        ids_in.share(ck.at[x, c], dev(xx(d), y, 1 - c))
    for d in range(1, Y):
        ids_in.share(cq.at[y], dev(x, yy(d), c))
    v_x, v_own = spread_keys(1)

    def sides(n, xo, co):
        rows = pl.ds(pl.multiple_of((xo * C + co) * T, T), T)
        block = kv[n, xo, co]
        kvc[n, rows, 0:H], kvc[n, rows, H:] = split(block)
        kvt[n, 0:H, rows], kvt[n, H:, rows] = split(jnp.transpose(block))

    sides(0, x, c)
    sides(1, x, c)
    k_own.wait_recv()
    sides(0, x, 1 - c)
    tree_g.step()
    tree_q.step()
    ids_in.wait_recv()

    def keys(i, _):
        xo, co = i // C, lax.rem(i, C)
        ckb[i] = jnp.transpose(jnp.broadcast_to(ck[xo, co][0:1, :], (T, T)))
        pkb[i] = dev(xo, y, co) * T + lax.broadcasted_iota(jnp.int32, (T, T), 0)
        return 0

    lax.fori_loop(0, X * C, keys, 0)

    def collect(n, across_x):
        over = []
        for d in (1, 3, 2):
            across_x[d].wait_recv()
            over.append((d, share(kv.at[n, xx(-d), c], sib)))
            sides(n, xx(-d), c)
        return over

    k_sib = collect(0, k_x)
    for d, copy in k_sib:
        copy.wait_recv()
        sides(0, xx(-d), 1 - c)
    tree_q.finish()

    KEYS = X * C * T

    def against(n, rows):
        hi, lo = split(rows)
        both = lax.dot_general(kvc[n], jnp.concatenate([hi, hi], axis=1), (NT, ((), ())), preferred_element_type=F32)
        return both + lax.dot_general(kvc[n, :, 0:H], lo, (NT, ((), ())), preferred_element_type=F32)

    def scores(i, _):
        s = against(0, qb[pl.ds(2 * i, 2)].reshape(2 * T, H)) * SCALE
        for n in range(2):
            o = 2 * i + n
            lanes = slice(n * T, (n + 1) * T)
            position = dev(x, o, c) * T + lax.broadcasted_iota(jnp.int32, (1, T), 1)
            same = ckb[...].reshape(KEYS, T) == cq[o][0:1, :]
            allowed = same & (pkb[...].reshape(KEYS, T) <= position)
            masked = jnp.where(allowed, s[:, lanes], NEG)
            top = jnp.max(masked, axis=0, keepdims=True)
            e = jnp.where(allowed, jnp.exp(masked - top), 0.0)
            eb[o] = e
            eh[i, :, lanes], el[i, :, lanes] = split(e)
            mlb[y, 0, pl.ds(o, 1), :] = top
            mlb[y, 1, pl.ds(o, 1), :] = jnp.sum(e, axis=0, keepdims=True)
        return 0

    lax.fori_loop(0, Y // 2, scores, 0)
    far_y = (4, 3, 5, 2, 6, 1, 7)
    ml_in, r_in = Batch(), Batch()
    for d in far_y:
        ml_in.share(mlb.at[y], dev(x, yy(d), c))
    v_own.wait_recv()
    sides(1, x, 1 - c)
    v_sib = collect(1, v_x)
    for d, copy in v_sib:
        copy.wait_recv()
        sides(1, xx(-d), 1 - c)
    tree_g.finish()

    def products(i, _):
        gv = against(1, gb[pl.ds(2 * i, 2)].reshape(2 * T, H))
        for n in range(2):
            o = 2 * i + n
            gvn = gv[:, n * T:(n + 1) * T]
            gvb[o] = gvn
            rb[y, pl.ds(o, 1), :] = jnp.sum(eb[o] * gvn, axis=0, keepdims=True)
        return 0

    lax.fori_loop(0, Y // 2, products, 0)
    for d in far_y:
        r_in.share(rb.at[y], dev(x, yy(d), c))

    ml_in.wait_recv()
    top = mlb[0, 0]
    for o in range(1, Y):
        top = jnp.maximum(top, mlb[o, 0])
    factors = [jnp.exp(mlb[o, 0] - top) for o in range(Y)]
    total = mlb[0, 1] * factors[0]
    for o in range(1, Y):
        total = total + mlb[o, 1] * factors[o]
    al_s[...] = jnp.exp(mlb[y, 0] - top) / total

    def scaled(i, _):
        for n in range(2):
            o = 2 * i + n
            rows = slice(n * T, (n + 1) * T)
            column = jnp.transpose(jnp.broadcast_to(al_s[pl.ds(o, 1), :], (T, T)))
            gsc[i, rows, 0:H], gsc[i, rows, H:] = split(gb[o] * column)
            qsc[i, rows, 0:H], qsc[i, rows, H:] = split(qb[o] * (column * SCALE))
        return 0

    lax.fori_loop(0, Y // 2, scaled, 0)

    def query_side(n, hi, lo, into, factor):
        def body(i, _):
            both = jnp.dot(kvt[n], hi[i], preferred_element_type=F32)
            r = both[0:H] + both[H:] + jnp.dot(kvt[n, 0:H], lo[i], preferred_element_type=F32)
            for m in range(2):
                o = 2 * i + m
                into[o] = r[:, m * T:(m + 1) * T] * (al_s[pl.ds(o, 1), :] * factor)
            return 0

        lax.fori_loop(0, Y // 2, body, 0)

    def key_side(n, d, hi, lo, with_):
        xo = xx(d)
        rows = pl.ds(pl.multiple_of(xo * (C * T), C * T), C * T)

        def add(i, acc):
            both = jnp.dot(hi[i, rows, :], with_[i], preferred_element_type=F32)
            rest = jnp.dot(lo[i, rows, :], with_[i, :, 0:H], preferred_element_type=F32)
            return acc + (both[:, 0:H] + both[:, H:] + rest)

        acc = lax.fori_loop(0, Y // 2, add, jnp.zeros((C * T, H), F32))
        gkv[n, xo] = acc.reshape(C, T, H)
        return start(gkv.at[n, xo, 1 - c], gsib.at[n, xo], sib)

    x_in = Batch()

    def key_send(n, d, copy):
        copy.wait_recv()
        gkv[n, xx(d), c] += gsib[n, xx(d)]
        if d:
            x_in.start(gkv.at[n, xx(d), c], gx.at[d - 1, n], dev(xx(d), y, c))

    query_side(1, eh, el, ob, 1.0)
    ring_o = Scatter(
        lambda o: ob.at[o], lambda o, h: ob.at[o, pl.ds(64 * h, 64)],
        lambda h, k: (obr, obl)[h].at[k], (obr.at[0, pl.ds(0, 64)], obl.at[0, pl.ds(64, 64)]),
    )
    far_x = (2, 1, 3, 0)
    last = None
    for d in far_x:
        copy = key_side(1, d, eh, el, gsc)
        if last is not None:
            key_send(1, *last)
        last = (d, copy)
    key_send(1, *last)
    ring_o.step(1)

    r_in.wait_recv()
    row = rb[0] * factors[0]
    for o in range(1, Y):
        row = row + rb[o] * factors[o]
    rr_s[...] = row / total

    def slopes(i, _):
        for n in range(2):
            o = 2 * i + n
            lanes = slice(n * T, (n + 1) * T)
            dh[i, :, lanes], dl[i, :, lanes] = split(eb[o] * (gvb[o] - rr_s[pl.ds(o, 1), :]))
        return 0

    lax.fori_loop(0, Y // 2, slopes, 0)

    last = (2, key_side(0, 2, dh, dl, qsc))
    query_side(0, dh, dl, gqb, SCALE)
    sum_q = Sum(
        lambda o: [gqb.at[o]], lambda o, h: [gqb.at[o, pl.ds(64 * h, 64)]],
        lambda h, k: [gq_in.at[h, k]], lambda h: [gq_half.at[h]],
    )
    sum_q.near()
    for d in far_x[1:]:
        copy = key_side(0, d, dh, dl, qsc)
        key_send(0, *last)
        last = (d, copy)
    sum_q.step()
    ring_o.step(2)
    key_send(0, *last)
    sum_q.finish()
    ring_o.step(3)
    x_in.wait_recv()
    parts = [jnp.transpose(gqb[y])]
    for n in range(2):
        parts.append((gkv[n, x, c] + gx[0, n]) + (gx[1, n] + gx[2, n]))
    grads = split(jnp.concatenate(parts, axis=1))

    y_order = (4, 3, -3, 2, -2, 1, -1, 0)

    def project(d):
        xo = xx(d)
        rows = pl.ds(pl.multiple_of(xo * (D // X), D // X), D // X)
        gw[xo] = dot3((toth[rows, :], totl[rows, :]), grads, NN).reshape(Y, C, 2, 16, 3 * H)
        return start(gw.at[xo, :, 1 - c], gws.at[xo], sib)

    def sum_for(*ds):
        return Sum(
            lambda o: [gw.at[xx(d), o, c, 0] for d in ds],
            lambda o, h: [gw.at[xx(d), o, c, 0, pl.ds(8 * h, 8)] for d in ds],
            lambda h, k: [(ga_r, ga_l)[h].at[d, k] for d in ds],
            lambda h: [(ga_r, ga_l)[h].at[d, 3, pl.ds(0, 8)] for d in ds],
        )

    bx_in = {n: Batch() for n in y_order}

    def launch(d, copy):
        copy.wait_recv()
        xo = xx(d)
        gw[xo, :, c] += gws[xo]
        if d:
            for n in y_order:
                o = yy(n)
                bx_in[n].start(gw.at[xo, o, c, 1], gbx.at[d - 1, o], dev(xo, y, c))

    first, second, third, fourth = [(d, project(d)) for d in far_x]
    launch(*first)
    launch(*second)
    sum_a = [sum_for(first[0], second[0])]
    launch(*third)
    launch(*fourth)
    sum_a.append(sum_for(third[0], fourth[0]))
    for tree in sum_a:
        tree.near()

    def gathered(*numbers):
        for n in numbers:
            o = yy(n)
            bx_in[n].wait_recv()
            gw[x, o, c, 1] += (gbx[0, o] + gbx[1, o]) + gbx[2, o]

    sum_a[0].step()
    gathered(4, 3, -3)
    sum_b = Sum(
        lambda o: [gw.at[x, o, c, 1]], lambda o, h: [gw.at[x, o, c, 1, pl.ds(8 * h, 8)]],
        lambda h, k: [(gb_r, gb_l)[h].at[k]], lambda h: [(gb_r, gb_l)[h].at[3, pl.ds(0, 8)]],
    )
    sum_a[1].step()
    gathered(2, -2)
    gathered(1, -1)
    sum_b.near()
    sum_b.step()
    gathered(0)
    a_in = Batch()
    for tree, pair in zip(sum_a, (far_x[:2], far_x[2:])):
        tree.finish()
        for d in pair:
            if d:
                a_in.start(gw.at[xx(d), y, c, 0], gax.at[d - 1], dev(xx(d), y, c))
    sum_b.finish()
    ring_o.step(4)
    att_o[...] = jnp.transpose(ob[y])
    grad_o[16:32, :] = gw[x, y, c, 1]
    a_in.wait_recv()
    grad_o[0:16, :] = (gw[x, y, c, 0] + gax[0]) + (gax[1] + gax[2])
    for i, rows in enumerate(sends):
        some = sizer.at[pl.ds(0, rows)]
        pltpu.make_async_copy(some, some, send.at[i]).wait()


def results(att, grad, att_o, gq_o, gk_o, gv_o):
    att_o[...] = att[...]
    for i, ref in enumerate((gq_o, gk_o, gv_o)):
        ref[...] = grad[:, i * H:(i + 1) * H]


def local(tokens, cluster, w_query, w_key, w_value, grad_out):
    vmem = pl.BlockSpec(memory_space=pltpu.VMEM)
    hbm = pl.BlockSpec(memory_space=pl.ANY)
    W3 = 3 * H
    keys = X * C * T
    pairs = Y // 2
    scratch = [
        pltpu.VMEM((T, D), F32),
        pltpu.VMEM((X, Y, C, 2, 16, W3), F32),
        pltpu.VMEM((T, D), BF16), pltpu.VMEM((T, D), BF16),
        pltpu.VMEM((D, T), BF16), pltpu.VMEM((D, T), BF16),
        pltpu.VMEM((Y, T, H), F32), pltpu.VMEM((Y, T, H), F32),
        pltpu.VMEM((2, X, C, T, H), F32),
        pltpu.VMEM((Y, 8, T), F32), pltpu.VMEM((X, C, 8, T), F32),
        pltpu.VMEM((X * C, T, T), F32), pltpu.VMEM((X * C, T, T), jnp.int32),
        pltpu.VMEM((2, keys, 2 * H), BF16), pltpu.VMEM((2, 2 * H, keys), BF16),
        pltpu.VMEM((pairs, 2 * T, 2 * H), BF16), pltpu.VMEM((pairs, 2 * T, 2 * H), BF16),
        pltpu.VMEM((Y, keys, T), F32), pltpu.VMEM((Y, keys, T), F32),
        pltpu.VMEM((pairs, keys, 2 * T), BF16), pltpu.VMEM((pairs, keys, 2 * T), BF16),
        pltpu.VMEM((pairs, keys, 2 * T), BF16), pltpu.VMEM((pairs, keys, 2 * T), BF16),
        pltpu.VMEM((Y, 2, Y, T), F32), pltpu.VMEM((Y, Y, T), F32),
        pltpu.VMEM((Y, T), F32), pltpu.VMEM((Y, T), F32),
        pltpu.VMEM((Y, H, T), F32),
        pltpu.VMEM((4, H, T), F32), pltpu.VMEM((4, H, T), F32),
        pltpu.VMEM((Y, H, T), F32),
        pltpu.VMEM((2, 3, H, T), F32), pltpu.VMEM((2, H // 2, T), F32),
        pltpu.VMEM((2, X, C, T, H), F32),
        pltpu.VMEM((2, X, T, H), F32),
        pltpu.VMEM((X - 1, 2, T, H), F32),
        pltpu.VMEM((X, Y, C, 2, 16, W3), F32),
        pltpu.VMEM((X, Y, 2, 16, W3), F32),
        pltpu.VMEM((X, 4, 16, W3), F32), pltpu.VMEM((X, 4, 16, W3), F32),
        pltpu.VMEM((X - 1, Y, 16, W3), F32),
        pltpu.VMEM((4, 16, W3), F32), pltpu.VMEM((4, 16, W3), F32),
        pltpu.VMEM((X - 1, 16, W3), F32),
        pltpu.VMEM((ROWS, 128), F32),
        pltpu.SemaphoreType.DMA((4,)),
        pltpu.SemaphoreType.DMA((COPIES,)),
        pltpu.SemaphoreType.DMA((8,)),
    ]
    att, grad = pl.pallas_call(
        kernel,
        out_shape=(
            jax.ShapeDtypeStruct((T, H), F32),
            jax.ShapeDtypeStruct((D // 64, W3), F32),
        ),
        in_specs=[hbm, vmem, hbm, hbm, hbm, hbm],
        out_specs=(vmem,) * 2,
        scratch_shapes=scratch,
        compiler_params=pltpu.CompilerParams(
            collective_id=0, has_side_effects=True, vmem_limit_bytes=58 * 1024 * 1024
        ),
        name="routing",
    )(tokens, cluster.reshape(1, T), w_query, w_key, w_value, grad_out)
    part = jax.ShapeDtypeStruct((D // 64, H), F32)
    return pl.pallas_call(
        results,
        out_shape=(jax.ShapeDtypeStruct((T, H), F32), part, part, part),
        in_specs=[vmem] * 2,
        out_specs=(vmem,) * 4,
        name="results",
    )(att, grad)


def solution(mesh):
    in_specs = (P("seq", None), P("seq", None)) + (P("seq", "head"),) * 4
    out_specs = (P("seq", "head"),) * 4
    return jax.shard_map(local, mesh=mesh, in_specs=in_specs, out_specs=out_specs, check_vma=False)
```

```python
import functools
import math

import jax
import jax.numpy as jnp
from jax import lax
from jax.experimental import pallas as pl
from jax.experimental.pallas import tpu as pltpu
from jax.sharding import PartitionSpec as P

MESH = pl.DeviceIdType.MESH
F32 = jnp.float32
BF16 = jnp.bfloat16
X, Y, C = 4, 8, 2
T = 128
H = 128
D = 2048
SCALE = 1.0 / math.sqrt(H)
NEG = -1e30
COPIES = 168
ROWS = 8192

NT = ((1,), (1,))
NN = ((1,), (0,))


def split(a):
    hi = a.astype(BF16)
    return hi, (a - hi.astype(F32)).astype(BF16)


def dot3(a, b, dims):
    def one(p, q):
        return lax.dot_general(p, q, (dims, ((), ())), preferred_element_type=F32)

    return one(a[0], b[0]) + (one(a[0], b[1]) + one(a[1], b[0]))


def kernel(
    tok_in, clu, wq, wk, wv, gout,
    att_o, grad_o,
    tok, wbuf, tokh, tokl, toth, totl, qb, gb, kv, cq, ck, ckb, pkb,
    kvc, kvt, qsc, gsc, eb, gvb, eh, el, dh, dl, mlb, rb, al_s, rr_s,
    ob, obr, obl, gqb, gq_in, gq_half, gkv, gsib, gx, gw, gws, ga_r, ga_l, gbx, gb_r, gb_l, gax,
    vw, vws, va_r, va_l, vbx, vb_r, vb_l, vax,
    sizer, send, recv, here,
):
    me = lax.axis_index("seq")
    c = lax.rem(me, C)
    y = lax.rem(me // C, Y)
    x = me // (C * Y)

    def yy(d):
        return lax.rem(y + (d + 2 * Y), Y)

    def xx(d):
        return lax.rem(x + (d + 2 * X), X)

    def dev(xd, yd, cd):
        return (xd * Y + yd) * C + cd

    right, left, sib = dev(x, yy(1), c), dev(x, yy(-1), c), dev(x, y, 1 - c)
    along = (1, right, 0), (-1, left, 1)
    groups = []
    sends = [0]

    class Batch:
        def __init__(self):
            self.rows, self.i = 0, len(groups)
            groups.append(self)

        def start(self, src, dst, device):
            rows = math.prod(src.shape) // 128
            if sends[-1] + rows > ROWS:
                sends.append(0)
            pltpu.make_async_remote_copy(
                src_ref=src, dst_ref=dst, send_sem=send.at[len(sends) - 1], recv_sem=recv.at[self.i],
                device_id={"seq": device}, device_id_type=MESH,
            ).start()
            sends[-1] += rows
            self.rows += rows
            return self

        def share(self, ref, device):
            return self.start(ref, ref, device)

        def wait_recv(self):
            some = sizer.at[pl.ds(0, self.rows)]
            pltpu.make_async_copy(some, some, recv.at[self.i]).wait()

    def start(src, dst, device):
        return Batch().start(src, dst, device)

    def share(ref, device):
        return Batch().share(ref, device)

    near = [dev(x, yy(d), c) for d in (1, -1, 2, -2)] + [dev(xx(d), y, c) for d in range(1, X)] + [sib]
    barrier = pltpu.get_barrier_semaphore()
    for peer in near:
        pl.semaphore_signal(barrier, inc=1, device_id={"seq": peer}, device_id_type=MESH)

    local_copies = []

    def fetch(src, dst):
        copy = pltpu.make_async_copy(src, dst, here.at[len(local_copies)])
        copy.start()
        local_copies.append(copy)

    for half in range(2):
        for i, ref in enumerate((wq, wk, wv)):
            fetch(ref.at[pl.ds(half * 16, 16), :], wbuf.at[x, y, c, half, :, pl.ds(i * H, H)])
    fetch(gout, gb.at[y])
    fetch(tok_in, tok)
    ids = jnp.broadcast_to(clu[...].astype(F32), (8, T))
    cq[y] = ids
    ck[x, c] = ids
    for copy in local_copies[:6]:
        copy.wait()
    pl.semaphore_wait(barrier, len(near))

    class Gather:
        def __init__(self, slots, halves):
            self.slots, self.halves = slots, halves
            self.two = [self.share(slots(y), dev(x, yy(2 * sign), c)) for sign, _, _ in along]
            self.one = [self.share(slots(y), to) for _, to, _ in along]

        def share(self, refs, device):
            batch = Batch()
            for ref in refs:
                batch.share(ref, device)
            return batch

        def step(self):
            self.far = []
            for (sign, to, h), copy in zip(along, self.two):
                copy.wait_recv()
                o = yy(-2 * sign)
                self.far.append(self.share(self.halves(o, h), dev(x, yy(2 * sign), c)))
                self.far.append(self.share(self.slots(o), to))
            for copy in self.one:
                copy.wait_recv()

        def finish(self):
            for copy in self.far:
                copy.wait_recv()

    class Sum:
        def __init__(self, parts, halves, into, into_half):
            self.parts, self.halves, self.into, self.into_half = parts, halves, into, into_half
            self.four = [
                self.start(halves(yy(4), h), into_half(h), dev(x, yy(2 * sign), c)) for sign, _, h in along
            ]
            self.three = [self.start(parts(yy(3 * sign)), into(h, 0), to) for sign, to, h in along]

        def start(self, src, dst, device):
            batch = Batch()
            for a, b in zip(src, dst):
                batch.start(a, b, device)
            return batch

        def step(self):
            self.two = []
            for (sign, _, h), four, three in zip(along, self.four, self.three):
                o = yy(2 * sign)
                four.wait_recv()
                for a, b in zip(self.halves(o, h), self.into_half(h)):
                    a[...] += b[...]
                three.wait_recv()
                for a, b in zip(self.parts(o), self.into(h, 0)):
                    a[...] += b[...]
                self.two.append(self.start(self.parts(o), self.into(h, 2), dev(x, yy(2 * sign), c)))

        def near(self):
            self.one = [self.start(self.parts(yy(sign)), self.into(h, 1), to) for sign, to, h in along]

        def finish(self):
            for copy in self.one + self.two:
                copy.wait_recv()
            for k in (1, 2):
                for h in (0, 1):
                    for a, b in zip(self.parts(y), self.into(h, k)):
                        a[...] += b[...]

    class Scatter:
        def __init__(self, part, half, into, into_half):
            self.part, self.half, self.into, self.into_half = part, half, into, into_half
            self.sent = [[start(half(yy(4), h), into_half[h], to)] for _, to, h in along]

        def step(self, k):
            for (sign, to, h), sent in zip(along, self.sent):
                sent[k - 1].wait_recv()
                o = yy(sign * (4 - k))
                mine = self.part(o)
                if k == 1:
                    first = self.half(o, h)
                    first[...] += self.into_half[h][...]
                else:
                    mine[...] += self.into(h, k - 1)[...]
                if k < 4:
                    sent.append(start(mine, self.into(h, k), to))

    def tree_for(*xs):
        return Gather(
            lambda o: [wbuf.at[i, o, c, 0] for i in xs],
            lambda o, h: [wbuf.at[i, o, c, 0, pl.ds(8 * h, 8)] for i in xs],
        )

    a_x = Batch()
    for d in (1, 3, 2):
        a_x.share(wbuf.at[x, y, c, 0], dev(xx(d), y, c))
    tree_own = tree_for(x)
    tree_b = Gather(lambda o: [wbuf.at[x, o, c, 1]], lambda o, h: [wbuf.at[x, o, c, 1, pl.ds(8 * h, 8)]])
    b_x = []
    sib_a, sib_b = Batch(), Batch()

    def spread(*numbers):
        for n in numbers:
            o, batch = yy(n), Batch()
            for d in (1, 3, 2):
                batch.share(wbuf.at[x, o, c, 1], dev(xx(d), y, c))
            b_x.append((o, batch))

    def across(count):
        for o, batch in b_x[:count]:
            batch.wait_recv()
            sib_b.share(wbuf.at[:, o, c, 1], sib)
        del b_x[:count]

    def over(*numbers):
        for n in numbers:
            sib_a.share(wbuf.at[:, yy(n), c, 0], sib)

    spread(0)
    local_copies[7].wait()

    def halves(i, _):
        cols = pl.ds(pl.multiple_of(i * 128, 128), 128)
        block = tok[:, cols]
        hi, lo = split(block)
        tokh[:, cols] = hi
        tokl[:, cols] = lo
        hi, lo = split(jnp.transpose(block))
        toth[cols, :] = hi
        totl[cols, :] = lo
        return 0

    lax.fori_loop(0, 8, halves, 0)
    local_copies[6].wait()
    a_x.wait_recv()
    tree_rest = tree_for(*[xx(d) for d in range(1, X)])
    over(0)
    tree_own.step()
    tree_b.step()
    spread(2, -2, 1, -1)
    lax.fori_loop(8, 12, halves, 0)
    across(1)
    tree_own.finish()
    tree_b.finish()
    spread(3, -3, 4)
    tree_rest.step()
    tree_g = Gather(lambda o: [gb.at[o]], lambda o, h: [gb.at[o, pl.ds(64 * h, 64)]])
    over(1, -1, 2, -2)
    across(4)
    lax.fori_loop(12, D // 128, halves, 0)
    tree_rest.finish()
    over(3, -3, 4)
    across(3)
    sib_a.wait_recv()
    sib_b.wait_recv()

    qkv = None
    for i in range(X):
        w = split(wbuf[i].reshape(D // X, 3 * H))
        cols = slice(i * (D // X), (i + 1) * (D // X))
        term = dot3((tokh[:, cols], tokl[:, cols]), w, NN)
        qkv = term if qkv is None else qkv + term
    qb[y] = qkv[:, 0:H]
    kv[0, x, c] = qkv[:, H:2 * H]
    kv[1, x, c] = qkv[:, 2 * H:]

    def spread_keys(n):
        across_x = {d: share(kv.at[n, x, c], dev(xx(d), y, c)) for d in (2, 1, 3)}
        return across_x, share(kv.at[n, x, c], sib)

    k_x, k_own = spread_keys(0)
    tree_q = Gather(lambda o: [qb.at[o]], lambda o, h: [qb.at[o, pl.ds(64 * h, 64)]])
    ids_in = Batch()
    for d in range(X):
        if d:
            ids_in.share(ck.at[x, c], dev(xx(d), y, c))
        ids_in.share(ck.at[x, c], dev(xx(d), y, 1 - c))
    for d in range(1, Y):
        ids_in.share(cq.at[y], dev(x, yy(d), c))
    v_x, v_own = spread_keys(1)

    def sides(n, xo, co):
        rows = pl.ds(pl.multiple_of((xo * C + co) * T, T), T)
        block = kv[n, xo, co]
        kvc[n, rows, 0:H], kvc[n, rows, H:] = split(block)
        kvt[n, 0:H, rows], kvt[n, H:, rows] = split(jnp.transpose(block))

    sides(0, x, c)
    sides(1, x, c)
    k_own.wait_recv()
    sides(0, x, 1 - c)
    tree_q.step()
    ids_in.wait_recv()

    def keys(i, _):
        xo, co = i // C, lax.rem(i, C)
        ckb[i] = jnp.transpose(jnp.broadcast_to(ck[xo, co][0:1, :], (T, T)))
        pkb[i] = dev(xo, y, co) * T + lax.broadcasted_iota(jnp.int32, (T, T), 0)
        return 0

    lax.fori_loop(0, X * C, keys, 0)

    def collect(n, across_x):
        over = []
        for d in (1, 3, 2):
            across_x[d].wait_recv()
            over.append((d, share(kv.at[n, xx(-d), c], sib)))
            sides(n, xx(-d), c)
        return over

    tree_g.step()
    k_sib = collect(0, k_x)
    for d, copy in k_sib:
        copy.wait_recv()
        sides(0, xx(-d), 1 - c)

    KEYS = X * C * T

    def pair(j):
        return lax.rem(y // 2 + j * (2 * lax.rem(y, 2) - 1) + 12, Y // 2)

    def pairs(body, first, last):
        lax.fori_loop(first, last, lambda j, carry: body(pair(j), carry), 0)

    def against(n, rows):
        hi, lo = split(rows)
        both = lax.dot_general(kvc[n], jnp.concatenate([hi, hi], axis=1), (NT, ((), ())), preferred_element_type=F32)
        return both + lax.dot_general(kvc[n, :, 0:H], lo, (NT, ((), ())), preferred_element_type=F32)

    def scores(i, _):
        s = against(0, qb[pl.ds(2 * i, 2)].reshape(2 * T, H)) * SCALE
        for n in range(2):
            o = 2 * i + n
            lanes = slice(n * T, (n + 1) * T)
            position = dev(x, o, c) * T + lax.broadcasted_iota(jnp.int32, (1, T), 1)
            same = ckb[...].reshape(KEYS, T) == cq[o][0:1, :]
            allowed = same & (pkb[...].reshape(KEYS, T) <= position)
            masked = jnp.where(allowed, s[:, lanes], NEG)
            top = jnp.max(masked, axis=0, keepdims=True)
            e = jnp.where(allowed, jnp.exp(masked - top), 0.0)
            eb[o] = e
            eh[i, :, lanes], el[i, :, lanes] = split(e)
            mlb[y, 0, pl.ds(o, 1), :] = top
            mlb[y, 1, pl.ds(o, 1), :] = jnp.sum(e, axis=0, keepdims=True)
        return 0

    pairs(scores, 0, 2)
    tree_q.finish()
    pairs(scores, 2, 4)
    far_y = (4, 3, 5, 2, 6, 1, 7)
    ml_in, r_in = Batch(), Batch()
    for d in far_y:
        ml_in.share(mlb.at[y], dev(x, yy(d), c))
    v_own.wait_recv()
    sides(1, x, 1 - c)
    v_sib = collect(1, v_x)
    for d, copy in v_sib:
        copy.wait_recv()
        sides(1, xx(-d), 1 - c)

    def products(i, _):
        gv = against(1, gb[pl.ds(2 * i, 2)].reshape(2 * T, H))
        for n in range(2):
            o = 2 * i + n
            gvn = gv[:, n * T:(n + 1) * T]
            gvb[o] = gvn
            rb[y, pl.ds(o, 1), :] = jnp.sum(eb[o] * gvn, axis=0, keepdims=True)
        return 0

    pairs(products, 0, 2)
    tree_g.finish()
    pairs(products, 2, 4)
    for d in far_y:
        r_in.share(rb.at[y], dev(x, yy(d), c))

    ml_in.wait_recv()
    top = mlb[0, 0]
    for o in range(1, Y):
        top = jnp.maximum(top, mlb[o, 0])
    factors = [jnp.exp(mlb[o, 0] - top) for o in range(Y)]
    total = mlb[0, 1] * factors[0]
    for o in range(1, Y):
        total = total + mlb[o, 1] * factors[o]
    al_s[...] = jnp.exp(mlb[y, 0] - top) / total

    def scaled(i, _):
        for n in range(2):
            o = 2 * i + n
            rows = slice(n * T, (n + 1) * T)
            column = jnp.transpose(jnp.broadcast_to(al_s[pl.ds(o, 1), :], (T, T)))
            gsc[i, rows, 0:H], gsc[i, rows, H:] = split(gb[o] * column)
            qsc[i, rows, 0:H], qsc[i, rows, H:] = split(qb[o] * (column * SCALE))
        return 0

    lax.fori_loop(0, Y // 2, scaled, 0)

    def query_side(n, hi, lo, into, factor, first, last):
        def body(i, _):
            both = jnp.dot(kvt[n], hi[i], preferred_element_type=F32)
            r = both[0:H] + both[H:] + jnp.dot(kvt[n, 0:H], lo[i], preferred_element_type=F32)
            for m in range(2):
                o = 2 * i + m
                into[o] = r[:, m * T:(m + 1) * T] * (al_s[pl.ds(o, 1), :] * factor)
            return 0

        pairs(body, first, last)

    def key_side(n, d, hi, lo, with_):
        xo = xx(d)
        rows = pl.ds(pl.multiple_of(xo * (C * T), C * T), C * T)

        def add(i, acc):
            both = jnp.dot(hi[i, rows, :], with_[i], preferred_element_type=F32)
            rest = jnp.dot(lo[i, rows, :], with_[i, :, 0:H], preferred_element_type=F32)
            return acc + (both[:, 0:H] + both[:, H:] + rest)

        acc = lax.fori_loop(0, Y // 2, add, jnp.zeros((C * T, H), F32))
        gkv[n, xo] = acc.reshape(C, T, H)
        return start(gkv.at[n, xo, 1 - c], gsib.at[n, xo], sib)

    x_in = [Batch(), Batch()]

    def key_send(n, d, copy):
        copy.wait_recv()
        gkv[n, xx(d), c] += gsib[n, xx(d)]
        if d:
            x_in[n].start(gkv.at[n, xx(d), c], gx.at[d - 1, n], dev(xx(d), y, c))

    far_x = (2, 1, 3, 0)
    last = None
    for d in far_x:
        copy = key_side(1, d, eh, el, gsc)
        if last is not None:
            key_send(1, *last)
        last = (d, copy)
    key_send(1, *last)

    r_in.wait_recv()
    row = rb[0] * factors[0]
    for o in range(1, Y):
        row = row + rb[o] * factors[o]
    rr_s[...] = row / total

    def slopes(i, _):
        for n in range(2):
            o = 2 * i + n
            lanes = slice(n * T, (n + 1) * T)
            dh[i, :, lanes], dl[i, :, lanes] = split(eb[o] * (gvb[o] - rr_s[pl.ds(o, 1), :]))
        return 0

    lax.fori_loop(0, Y // 2, slopes, 0)

    y_order = (4, 3, -3, 2, -2, 1, -1, 0)

    class Weight:
        def __init__(self, buf, from_sib, a_r, a_l, bx, b_r, b_l, ax):
            self.buf, self.from_sib, self.a, self.bx = buf, from_sib, (a_r, a_l), bx
            self.b, self.ax = (b_r, b_l), ax
            self.width = buf.shape[-1]

        def project(self, d, grads):
            xo = xx(d)
            rows = pl.ds(pl.multiple_of(xo * (D // X), D // X), D // X)
            part = dot3((toth[rows, :], totl[rows, :]), grads, NN)
            self.buf[xo] = part.reshape(Y, C, 2, 16, self.width)
            return d, start(self.buf.at[xo, :, 1 - c], self.from_sib.at[xo], sib)

        def launch(self, d, copy):
            copy.wait_recv()
            xo = xx(d)
            self.buf[xo, :, c] += self.from_sib[xo]
            if d:
                for n in y_order:
                    o = yy(n)
                    self.bx_in[n].start(self.buf.at[xo, o, c, 1], self.bx.at[d - 1, o], dev(xo, y, c))

        def sum_for(self, *ds):
            return Sum(
                lambda o: [self.buf.at[xx(d), o, c, 0] for d in ds],
                lambda o, h: [self.buf.at[xx(d), o, c, 0, pl.ds(8 * h, 8)] for d in ds],
                lambda h, k: [self.a[h].at[d, k] for d in ds],
                lambda h: [self.a[h].at[d, 3, pl.ds(0, 8)] for d in ds],
            )

        def begin(self, grads):
            self.bx_in = {n: Batch() for n in y_order}
            made = [self.project(d, grads) for d in far_x]
            self.launch(*made[0])
            self.launch(*made[1])
            self.sum_a = [self.sum_for(*far_x[:2])]
            self.launch(*made[2])
            self.launch(*made[3])
            self.sum_a.append(self.sum_for(*far_x[2:]))
            for tree in self.sum_a:
                tree.near()

        def gathered(self, *numbers):
            for n in numbers:
                o = yy(n)
                self.bx_in[n].wait_recv()
                self.buf[x, o, c, 1] += (self.bx[0, o] + self.bx[1, o]) + self.bx[2, o]

        def first(self):
            self.sum_a[0].step()
            self.gathered(4, 3, -3)
            self.sum_b = Sum(
                lambda o: [self.buf.at[x, o, c, 1]], lambda o, h: [self.buf.at[x, o, c, 1, pl.ds(8 * h, 8)]],
                lambda h, k: [self.b[h].at[k]], lambda h: [self.b[h].at[3, pl.ds(0, 8)]],
            )

        def second(self):
            self.sum_a[1].step()
            self.gathered(2, -2, 1, -1)
            self.sum_b.near()

        def third(self):
            self.sum_b.step()
            self.gathered(0)

        def late(self):
            self.a_in = Batch()
            for tree, pair in zip(self.sum_a, (far_x[:2], far_x[2:])):
                tree.finish()
                for d in pair:
                    if d:
                        self.a_in.start(self.buf.at[xx(d), y, c, 0], self.ax.at[d - 1], dev(xx(d), y, c))
            self.sum_b.finish()

        def result(self, lanes):
            grad_o[16:32, lanes] = self.buf[x, y, c, 1]
            self.a_in.wait_recv()
            ax = self.ax
            grad_o[0:16, lanes] = (self.buf[x, y, c, 0] + ax[0]) + (ax[1] + ax[2])

    def key_total(n):
        x_in[n].wait_recv()
        return (gkv[n, x, c] + gx[0, n]) + (gx[1, n] + gx[2, n])

    w_qk = Weight(gw, gws, ga_r, ga_l, gbx, gb_r, gb_l, gax)
    w_v = Weight(vw, vws, va_r, va_l, vbx, vb_r, vb_l, vax)

    last = (2, key_side(0, 2, dh, dl, qsc))
    query_side(0, dh, dl, gqb, SCALE, 2, 4)
    sum_q = Sum(
        lambda o: [gqb.at[o]], lambda o, h: [gqb.at[o, pl.ds(64 * h, 64)]],
        lambda h, k: [gq_in.at[h, k]], lambda h: [gq_half.at[h]],
    )
    query_side(0, dh, dl, gqb, SCALE, 0, 2)
    sum_q.near()
    w_v.begin(split(key_total(1)))
    copy = key_side(0, far_x[1], dh, dl, qsc)
    key_send(0, *last)
    last = (far_x[1], copy)
    for d in far_x[2:]:
        copy = key_side(0, d, dh, dl, qsc)
        key_send(0, *last)
        last = (d, copy)
    key_send(0, *last)
    sum_q.step()
    query_side(1, eh, el, ob, 1.0, 0, 4)
    ring_o = Scatter(
        lambda o: ob.at[o], lambda o, h: ob.at[o, pl.ds(64 * h, 64)],
        lambda h, k: (obr, obl)[h].at[k], (obr.at[0, pl.ds(0, 64)], obl.at[0, pl.ds(64, 64)]),
    )
    w_v.first()
    w_v.second()
    sum_q.finish()
    ring_o.step(1)
    w_qk.begin(split(jnp.concatenate([jnp.transpose(gqb[y]), key_total(0)], axis=1)))
    w_v.third()
    ring_o.step(2)
    w_qk.first()
    w_v.late()
    w_qk.second()
    ring_o.step(3)
    w_qk.third()
    w_qk.late()
    w_v.result(slice(2 * H, 3 * H))
    w_qk.result(slice(0, 2 * H))
    ring_o.step(4)
    att_o[...] = jnp.transpose(ob[y])
    for i, rows in enumerate(sends):
        some = sizer.at[pl.ds(0, rows)]
        pltpu.make_async_copy(some, some, send.at[i]).wait()


def results(att, grad, att_o, gq_o, gk_o, gv_o):
    att_o[...] = att[...]
    for i, ref in enumerate((gq_o, gk_o, gv_o)):
        ref[...] = grad[:, i * H:(i + 1) * H]


def local(tokens, cluster, w_query, w_key, w_value, grad_out):
    vmem = pl.BlockSpec(memory_space=pltpu.VMEM)
    hbm = pl.BlockSpec(memory_space=pl.ANY)
    W3 = 3 * H
    keys = X * C * T
    pairs = Y // 2
    sums = []
    scratch = [
        pltpu.VMEM((T, D), F32),
        pltpu.VMEM((X, Y, C, 2, 16, W3), F32),
        pltpu.VMEM((T, D), BF16), pltpu.VMEM((T, D), BF16),
        pltpu.VMEM((D, T), BF16), pltpu.VMEM((D, T), BF16),
        pltpu.VMEM((Y, T, H), F32), pltpu.VMEM((Y, T, H), F32),
        pltpu.VMEM((2, X, C, T, H), F32),
        pltpu.VMEM((Y, 8, T), F32), pltpu.VMEM((X, C, 8, T), F32),
        pltpu.VMEM((X * C, T, T), F32), pltpu.VMEM((X * C, T, T), jnp.int32),
        pltpu.VMEM((2, keys, 2 * H), BF16), pltpu.VMEM((2, 2 * H, keys), BF16),
        pltpu.VMEM((pairs, 2 * T, 2 * H), BF16), pltpu.VMEM((pairs, 2 * T, 2 * H), BF16),
        pltpu.VMEM((Y, keys, T), F32), pltpu.VMEM((Y, keys, T), F32),
        pltpu.VMEM((pairs, keys, 2 * T), BF16), pltpu.VMEM((pairs, keys, 2 * T), BF16),
        pltpu.VMEM((pairs, keys, 2 * T), BF16), pltpu.VMEM((pairs, keys, 2 * T), BF16),
        pltpu.VMEM((Y, 2, Y, T), F32), pltpu.VMEM((Y, Y, T), F32),
        pltpu.VMEM((Y, T), F32), pltpu.VMEM((Y, T), F32),
        pltpu.VMEM((Y, H, T), F32),
        pltpu.VMEM((4, H, T), F32), pltpu.VMEM((4, H, T), F32),
        pltpu.VMEM((Y, H, T), F32),
        pltpu.VMEM((2, 3, H, T), F32), pltpu.VMEM((2, H // 2, T), F32),
        pltpu.VMEM((2, X, C, T, H), F32),
        pltpu.VMEM((2, X, T, H), F32),
        pltpu.VMEM((X - 1, 2, T, H), F32),
        pltpu.VMEM((ROWS, 128), F32),
        pltpu.SemaphoreType.DMA((4,)),
        pltpu.SemaphoreType.DMA((COPIES,)),
        pltpu.SemaphoreType.DMA((8,)),
    ]
    for wide in (2 * H, H):
        ring = pltpu.VMEM((X, 4, 16, wide), F32)
        small = pltpu.VMEM((4, 16, wide), F32)
        sums += [
            pltpu.VMEM((X, Y, C, 2, 16, wide), F32), pltpu.VMEM((X, Y, 2, 16, wide), F32), ring, ring,
            pltpu.VMEM((X - 1, Y, 16, wide), F32), small, small, pltpu.VMEM((X - 1, 16, wide), F32),
        ]
    scratch[-4:-4] = sums
    att, grad = pl.pallas_call(
        kernel,
        out_shape=(
            jax.ShapeDtypeStruct((T, H), F32),
            jax.ShapeDtypeStruct((D // 64, W3), F32),
        ),
        in_specs=[hbm, vmem, hbm, hbm, hbm, hbm],
        out_specs=(vmem,) * 2,
        scratch_shapes=scratch,
        compiler_params=pltpu.CompilerParams(
            collective_id=0, has_side_effects=True, vmem_limit_bytes=58 * 1024 * 1024
        ),
        name="routing",
    )(tokens, cluster.reshape(1, T), w_query, w_key, w_value, grad_out)
    part = jax.ShapeDtypeStruct((D // 64, H), F32)
    return pl.pallas_call(
        results,
        out_shape=(jax.ShapeDtypeStruct((T, H), F32), part, part, part),
        in_specs=[vmem] * 2,
        out_specs=(vmem,) * 4,
        name="results",
    )(att, grad)


def solution(mesh):
    in_specs = (P("seq", None), P("seq", None)) + (P("seq", "head"),) * 4
    out_specs = (P("seq", "head"),) * 4
    return jax.shard_map(local, mesh=mesh, in_specs=in_specs, out_specs=out_specs, check_vma=False)
```
